32 devices in a mesh: tm: 8 (over z, x), blk: 4 (over y, core).
Axes of the slice: x: 2, y: 2, z: 4, core: 2. Of those that a mesh axis runs over, the one named last changes fastest.
Arguments:
- prior_mean: float32 [512], replicated, may hold values from -6 to 6
- after_mean: float32 [512], replicated, may hold values from -6 to 6
- filter_map: float32 [16, 512, 512], P('tm', 'blk'), may hold values from -1 to 1.5
- smoother_gain: float32 [16, 512, 512], P('tm', 'blk'), may hold values from -1 to 1.5
- smoother_map: float32 [16, 512, 512], P('tm', 'blk'), may hold values from -1 to 1.5
- obs_gain: float32 [16, 512, 128], P('tm', 'blk'), may hold values from -0.5 to 0.5
- observations: float32 [16, 128], P('tm'), may hold values from -6 to 6
Outputs:
- filtered: float32 [16, 512], P('tm', 'blk')
- smoothed: float32 [16, 512], P('tm', 'blk')
The draws below stay inside these ranges and needn't reach their ends.
All inputs are finite; a program needn't handle non-finite values.
Results may differ from the reference program's by a relative error of at most 0.0003.
Values sent between devices are 32-bit elements; how exact they have to be, the bound alone decides.
No kernel may reach another device: no remote copies, remote signals or barrier semaphores. Data moves between devices by JAX's collectives and lax.ppermute only.
A program may use at most 128 MiB of HBM per device.

```python
import math
import jax
import jax.numpy as jnp
from jax import lax

LATENT_SIZE = 512
OBS = 128
HORIZON_LENGTH = 16


def decaying_map(key, lasting_share, mixing_size):
    sampler_seeds = jax.random.split(key, 7)
    lasting = jax.random.uniform(sampler_seeds[0], (LATENT_SIZE,)) < lasting_share
    fast_forget = jax.random.uniform(sampler_seeds[1], (LATENT_SIZE,), minval=0.06, maxval=0.12)
    slow_forget = jax.random.uniform(sampler_seeds[2], (LATENT_SIZE,), minval=0.01, maxval=0.025)
    forget = jnp.where(lasting, slow_forget, fast_forget)
    factor = jax.random.uniform(sampler_seeds[3], (HORIZON_LENGTH, LATENT_SIZE), minval=0.5, maxval=1.5)
    kept_entries = 1.0 - forget[None, :] * factor
    segment_batches = jax.random.randint(sampler_seeds[4], (3,), 0, HORIZON_LENGTH)
    segment_spacing = jnp.any(jnp.arange(HORIZON_LENGTH)[:, None] == segment_batches[None, :], axis=1)
    segment_limit = jax.random.uniform(sampler_seeds[5], (HORIZON_LENGTH, LATENT_SIZE), minval=0.5, maxval=0.8)
    kept_entries = jnp.where(segment_spacing[:, None], kept_entries * segment_limit, kept_entries)
    mixing = jax.random.truncated_normal(sampler_seeds[6], -4.0, 4.0, (HORIZON_LENGTH, LATENT_SIZE, LATENT_SIZE)) * (mixing_size / math.sqrt(LATENT_SIZE))
    return (mixing + kept_entries[:, :, None] * jnp.eye(LATENT_SIZE, dtype=jnp.float32)[None]).astype(jnp.float32)


def draw_filter_map(key, part):
    return decaying_map(jax.random.fold_in(key, 3), 0.5, 0.2)


def draw_smoother_gain(key, part):
    return decaying_map(jax.random.fold_in(key, 11), 0.5, 0.2)


def draw_smoother_map(key, part):
    sampler_seeds = jax.random.split(jax.random.fold_in(key, 19), 2)
    diagonal = jax.random.uniform(sampler_seeds[0], (HORIZON_LENGTH, LATENT_SIZE), minval=0.4, maxval=1.0)
    mixing = jax.random.truncated_normal(sampler_seeds[1], -4.0, 4.0, (HORIZON_LENGTH, LATENT_SIZE, LATENT_SIZE)) * (0.3 / math.sqrt(LATENT_SIZE))
    return (mixing + diagonal[:, :, None] * jnp.eye(LATENT_SIZE, dtype=jnp.float32)[None]).astype(jnp.float32)


def block_scale(rng, shape, cuts, least, high):
    level = 1.0
    for position, blocks in cuts:
        draws = jax.random.uniform(jax.random.fold_in(jax.random.fold_in(rng, 6), position), (blocks,), jnp.float32, least / len(cuts), high / len(cuts))
        level = level * jnp.repeat(jnp.exp(draws), shape[position] // blocks).reshape((-1,) + (1,) * (len(shape) - 1 - position))
    return level


def gaussian(stream_key, shape, spread, most, shards=(), kind=jnp.bfloat16):
    result = spread * jax.random.normal(stream_key, shape, jnp.float32)
    if shards:
        result = result * block_scale(stream_key, shape, shards, -0.22, 0.18)
    return jnp.clip(result, -most, most).astype(kind)


def setup_inputs(seed: int = 0) -> dict:
    arg_keys = jax.random.split(jax.random.key(seed), 8)
    return {
        "prior_mean": gaussian(arg_keys[0], (LATENT_SIZE,), 1.0, 6.0, (), jnp.float32),
        "after_mean": gaussian(arg_keys[1], (LATENT_SIZE,), 1.0, 6.0, (), jnp.float32),
        "filter_map": draw_filter_map(jax.random.fold_in(arg_keys[7], 71), 0),
        "smoother_gain": draw_smoother_gain(jax.random.fold_in(arg_keys[7], 71), 0),
        "smoother_map": draw_smoother_map(jax.random.fold_in(arg_keys[7], 71), 0),
        "obs_gain": gaussian(arg_keys[5], (HORIZON_LENGTH, LATENT_SIZE, OBS), OBS ** -0.5, 0.5, ((0, 8), (1, 4)), jnp.float32),
        "observations": gaussian(arg_keys[6], (HORIZON_LENGTH, OBS), 1.0, 6.0, ((0, 8),), jnp.float32),
    }


def reference(prior_mean, after_mean, filter_map, smoother_gain, smoother_map, obs_gain, observations):
    highest = lax.Precision.HIGHEST
    drive = jnp.einsum("tso,to->ts", obs_gain, observations, precision=highest)

    def forward(current, inputs):
        step_map, offset = inputs
        current = jnp.dot(step_map, current, precision=highest) + offset
        return current, current

    ignored, filtered = lax.scan(forward, prior_mean, (filter_map, drive))
    pulled = jnp.einsum("tsk,tk->ts", smoother_map, filtered, precision=highest)

    def backward(current, inputs):
        step_gain, offset = inputs
        current = jnp.dot(step_gain, current, precision=highest) + offset
        return current, current

    unused, smoothed = lax.scan(backward, after_mean, (smoother_gain, pulled), reverse=True)
    return filtered, smoothed
```

```python
import functools

import jax
import jax.numpy as jnp
from jax import lax
from jax.experimental import pallas as pl
from jax.experimental.pallas import tpu as pltpu
from jax.sharding import PartitionSpec as P

LANES = 128


def flip(value, bit_mask, size):
    result = 0
    weight = 1
    while weight < size:
        bit = lax.rem(lax.div(value, weight), 2)
        if bit_mask & weight:
            bit = 1 - bit
        result = result + bit * weight
        weight = weight * 2
    return result


def partner(value, tm_mask, blk_mask):
    count = lax.axis_size("tm")
    blocks = lax.axis_size("blk")
    pairs = [
        (t * blocks + b, (t ^ tm_mask) * blocks + (b ^ blk_mask))
        for t in range(count)
        for b in range(blocks)
    ]
    return lax.ppermute(value, ("tm", "blk"), pairs)


def collect(value, merge):
    blocks = lax.axis_size("blk")
    held = {}
    far = [(a, m) for a in range(merge) for m in range(0, blocks, 2)]
    for a, m in far:
        held[a, m] = value if (a, m) == (0, 0) else partner(value, a, m)
    for a, m in far:
        held[a, m + 1] = partner(held[a, m], 0, 1)
    return held


def stage_kernel(stage, merge, steps, forward, masks, *refs):
    pieces = refs[: len(masks)]
    offsets = refs[len(masks) : 2 * len(masks)]
    refs = refs[2 * len(masks) :]
    if forward:
        map_ref, entering_ref, kept_ref, kept_own_ref = refs[:4]
        out_ref, own_ref, last_ref = refs[4:7]
        held, local, sems, local_sem = refs[7:]
    else:
        entering_ref, kept_own_ref, own_ref, last_ref = refs[:4]
        held, sems = refs[4:]
    index = lax.axis_index("tm")
    place = lax.axis_index("blk")
    blocks = lax.axis_size("blk")
    group = lax.div(index, merge)
    side = lax.rem(index, merge)
    rows = held.shape[2]
    width = held.shape[3]
    tiles = width // LANES
    row_tiles = rows // LANES
    total = merge * steps

    @pl.when(group != stage)
    def _():
        own_ref[...] = kept_own_ref[...]
        last_ref[...] = entering_ref[...]
        if forward:
            out_ref[...] = kept_ref[...]

    @pl.when(group == stage)
    def _():
        copies = {}
        for number, (a, m) in enumerate(masks):
            at = flip(side, a, merge) * steps
            for s in range(steps):
                copies[number, s] = pltpu.make_async_copy(
                    pieces[number].at[s], held.at[at + s, m], sems.at[at + s, m]
                )
        order = range(steps) if forward else range(steps - 1, -1, -1)
        for s in order:
            for number in range(len(masks)):
                copies[number, s].start()
        if forward:
            local_copy = pltpu.make_async_copy(map_ref, local, local_sem)
            local_copy.start()

        def matvec(matrix, vector):
            acc = matrix[:, 0:LANES] * vector[0:1, :]
            for c in range(1, tiles):
                acc = acc + matrix[:, c * LANES : (c + 1) * LANES] * vector[c : c + 1, :]
            return [
                jnp.sum(acc[r * LANES : (r + 1) * LANES, :].T, axis=0, keepdims=True)
                for r in range(row_tiles)
            ]

        last_ref[...] = entering_ref[...]
        for number in range(total):
            t = number if forward else total - 1 - number
            a_here = t // steps
            s = t % steps
            for m in range(blocks):
                pltpu.make_async_copy(pieces[0].at[0], held.at[t, m], sems.at[t, m]).wait()
            vector = last_ref[...]
            for m in range(blocks):
                parts = matvec(held[t, m], vector)
                where = flip(place, m, blocks) * row_tiles
                near = offsets[masks.index((0, m))]
                add = near[s]
                if merge == 2:
                    far = offsets[masks.index((1, m))]
                    add = jnp.where(side == a_here, near[s], far[s])
                for r in range(row_tiles):
                    value = parts[r] + add[r : r + 1, :]
                    last_ref[pl.ds(where + r, 1), :] = value
                    if forward:
                        out_ref[t, pl.ds(where + r, 1), :] = value
                    if m == 0:
                        own_at = (0, s) if forward else (s,)

                        @pl.when(side == a_here)
                        def _():
                            own_ref[own_at + (slice(r, r + 1), slice(None))] = value
        if forward:
            local_copy.wait()
            for s in range(steps):
                mean = out_ref[side * steps + s]
                parts = matvec(local[s], mean)
                for r in range(row_tiles):
                    own_ref[1, s, r : r + 1, :] = parts[r]


def shards(prior_mean, after_mean, filter_map, smoother_gain, smoother_map, obs_gain, observations):
    highest = lax.Precision.HIGHEST
    steps, rows, width = filter_map.shape
    count = lax.axis_size("tm")
    blocks = lax.axis_size("blk")
    merge = 2 if count % 2 == 0 else 1
    stages = count // merge
    total = merge * steps
    tiles = width // LANES
    row_tiles = rows // LANES
    masks = [(a, m) for a in range(merge) for m in range(blocks)]

    drive_rows = jnp.einsum("tro,to->tr", obs_gain, observations, precision=highest)
    maps = collect(filter_map, merge)
    drives = collect(drive_rows.reshape(steps, row_tiles, LANES), merge)
    gains = collect(smoother_gain, merge)

    anywhere = pl.BlockSpec(memory_space=pl.ANY)
    in_vmem = pl.BlockSpec(memory_space=pltpu.VMEM)
    mean_shape = jax.ShapeDtypeStruct((tiles, LANES), jnp.float32)
    group_shape = jax.ShapeDtypeStruct((total, tiles, LANES), jnp.float32)
    own_shape = jax.ShapeDtypeStruct((steps, row_tiles, LANES), jnp.float32)
    both_shape = jax.ShapeDtypeStruct((2, steps, row_tiles, LANES), jnp.float32)
    held = pltpu.VMEM((total, blocks, rows, width), jnp.float32)
    sems = pltpu.SemaphoreType.DMA((total, blocks))

    def hop(value, source, target):
        pairs = [
            ((source * merge + x) * blocks + b, (target * merge + x) * blocks + b)
            for x in range(merge)
            for b in range(blocks)
        ]
        return lax.ppermute(value, ("tm", "blk"), pairs)

    out = jnp.zeros(group_shape.shape, jnp.float32)
    own = jnp.zeros(both_shape.shape, jnp.float32)
    vector = prior_mean.reshape(tiles, LANES)
    for stage in range(stages):
        out, own, vector = pl.pallas_call(
            functools.partial(stage_kernel, stage, merge, steps, True, masks),
            out_shape=(group_shape, both_shape, mean_shape),
            in_specs=[anywhere] * len(masks) + [in_vmem] * len(masks) + [anywhere] + [in_vmem] * 3,
            out_specs=(in_vmem,) * 3,
            scratch_shapes=[held, pltpu.VMEM((steps, rows, width), jnp.float32), sems, pltpu.SemaphoreType.DMA],
            name=f"forward_{stage}",
        )(*[maps[k] for k in masks], *[drives[k] for k in masks], smoother_map, vector, out, own)
        if stage < stages - 1:
            vector = hop(vector, stage, stage + 1)
    filtered_rows = own[0].reshape(steps, rows)
    pulled = collect(own[1], merge)

    own = jnp.zeros(own_shape.shape, jnp.float32)
    vector = after_mean.reshape(tiles, LANES)
    for stage in range(stages - 1, -1, -1):
        own, vector = pl.pallas_call(
            functools.partial(stage_kernel, stage, merge, steps, False, masks),
            out_shape=(own_shape, mean_shape),
            in_specs=[anywhere] * len(masks) + [in_vmem] * len(masks) + [in_vmem] * 2,
            out_specs=(in_vmem,) * 2,
            scratch_shapes=[held, sems],
            name=f"backward_{stage}",
        )(*[gains[k] for k in masks], *[pulled[k] for k in masks], vector, own)
        if stage > 0:
            vector = hop(vector, stage, stage - 1)
    return (filtered_rows, own.reshape(steps, rows))


def solution(mesh):
    placed = (
        P(),
        P(),
        P("tm", "blk", None),
        P("tm", "blk", None),
        P("tm", "blk", None),
        P("tm", "blk", None),
        P("tm", None),
    )
    return jax.shard_map(
        shards,
        mesh=mesh,
        in_specs=placed,
        out_specs=(P("tm", "blk"), P("tm", "blk")),
        check_vma=False,
    )
```
